32 devices in a mesh: slab: 8 (over y, x, core), col: 4 (over z).
Axes of the slice: x: 2, y: 2, z: 4, core: 2. Of those that a mesh axis runs over, the one named last changes fastest.
Arguments:
- volume: bfloat16 [8, 512, 6144], P('slab', 'col'), may hold values from -6 to 6
- detector_row_weight: bfloat16 [8, 512], P(None, 'col'), may hold values from -0.25 to 0.25
- tile_bank: bfloat16 [4, 128, 128], replicated, may hold values from -0.5 to 0.5
- tile_class: int32 [8], replicated, may hold values from 0 to 3
- tile_shift: int32 [8], replicated, may hold values from 0 to 47
- owner_angle: int32 [8], replicated, may hold values from 0 to 7, each once
- measured: bfloat16 [8, 8, 6144], P('slab', None, 'col'), may hold values from -6 to 6
- window_slice: int32 [8], P('slab'), may hold values from -4 to 0
- window_col: int32 [8], P('slab'), may hold values from -32 to 16
Outputs:
- projection: bfloat16 [8, 8, 6144], P('slab', None, 'col')
- correlation: float32 [8, 4, 16], P('slab')
- shifts: float32 [2, 8], P(None, 'slab')
The draws below stay inside these ranges and needn't reach their ends.
Inputs may be any that keep to these rules, and one draw needn't show every extreme that they name: `owner_angle`: every angle stands in exactly one slot.
All inputs are finite; a program needn't handle non-finite values.
Results may differ from the reference program's by a relative error of at most 0.0095.
Values may be sent and summed in bfloat16 or wider, within the bound.
A program may use at most 64 MiB of HBM per device.

```python
import math
import jax
import jax.numpy as jnp
from jax import lax

NU = 6144
TILE = 128
NB = 4
RW = 512
LAG = 32
WU = 16
LAGZ = 4
WZ = 4
NT = 48
RQ = 128
NZ = 8
ANG = 8
N_COL = 4


def plant(result, rng, smallest, top_value):
    dims = result.shape
    place = [jax.random.randint(jax.random.fold_in(rng, axis), (), 0, dims[axis]) for axis in range(len(dims))]
    result = result.at[tuple(place)].set(smallest)
    longest = dims.index(max(dims))
    place[longest] = (place[longest] + 1) % dims[longest]
    return result.at[tuple(place)].set(top_value)


def block_levels(stream_key, shape, split, least, top_value):
    gain, own = 1.0, jax.random.fold_in(stream_key, 6)
    for position, parts in split:
        draws = jnp.exp(jax.random.uniform(jax.random.fold_in(own, position), (parts,), jnp.float32, least / len(split), top_value / len(split)))
        gain = gain * jnp.repeat(draws, shape[position] // parts).reshape([-1 if axis == position else 1 for axis in range(len(shape))])
    return gain


def scatter_about(key, extent, scale, most, pieces=(), held_as=jnp.bfloat16):
    drawn = jax.random.normal(key, extent, jnp.float32) * scale
    if len(pieces) > 0:
        drawn = block_levels(key, extent, pieces, -0.22, 0.18) * drawn
    return jnp.clip(drawn, min=-most, max=most).astype(held_as)


def setup_inputs(seed: int = 0) -> dict:
    streams_of = jax.random.split(jax.random.key(seed), 10)
    return {
        "volume": scatter_about(streams_of[0], (NZ, RW, NU), 1.0, 6.0, ((0, 8), (1, 4))),
        "detector_row_weight": scatter_about(streams_of[1], (ANG, RW), RW ** -0.5, 0.25, ((1, 4),)),
        "tile_bank": scatter_about(streams_of[2], (NB, TILE, TILE), TILE ** -0.5, 0.5),
        "tile_class": plant(jax.random.randint(streams_of[3], (ANG,), 0, NB), jax.random.fold_in(streams_of[3], 1), 0, NB - 1).astype(jnp.int32),
        "tile_shift": plant(jax.random.randint(streams_of[4], (ANG,), 0, NT), jax.random.fold_in(streams_of[4], 1), 0, NT - 1).astype(jnp.int32),
        "owner_angle": jax.random.permutation(streams_of[5], ANG).astype(jnp.int32),
        "measured": scatter_about(streams_of[6], (ANG, NZ, NU), 1.0, 6.0, ((0, 8), (2, 4))),
        "window_slice": plant(jax.random.randint(streams_of[7], (ANG,), 0 - LAGZ, LAGZ - WZ + 1), jax.random.fold_in(streams_of[7], 1), 0 - LAGZ, LAGZ - WZ).astype(jnp.int32),
        "window_col": plant(jax.random.randint(streams_of[8], (ANG,), 0 - LAG, LAG - WU + 1), jax.random.fold_in(streams_of[8], 1), 0 - LAG, LAG - WU).astype(jnp.int32),
    }


def reference(volume, detector_row_weight, tile_bank, tile_class, tile_shift, owner_angle, measured, window_slice, window_col):
    chosen = jnp.take(detector_row_weight, owner_angle, axis=0).astype(jnp.float32)
    shift_chosen = jnp.take(tile_shift, owner_angle)
    system_operators = jnp.take(tile_bank, jnp.take(tile_class, owner_angle), axis=0).astype(jnp.float32)
    targets = jnp.arange(NT, dtype=jnp.int32)
    sources = ((targets[None, :] - shift_chosen[:, None]) % NT).astype(jnp.int32)

    def project_plane(plane):
        plane_wide = plane.astype(jnp.float32)
        summed = jnp.zeros((ANG, NU), jnp.float32)
        for block_index in range(N_COL):
            lower = block_index * RQ
            ray_sums = jnp.dot(chosen[:, lower:lower + RQ], plane_wide[lower:lower + RQ], precision=lax.Precision.HIGHEST, preferred_element_type=jnp.float32).astype(jnp.bfloat16)
            rolled = jnp.take_along_axis(ray_sums.reshape(ANG, NT, TILE), sources[:, :, None], axis=1)
            spread = jnp.einsum('ktc,kcd->ktd', rolled.astype(jnp.float32), system_operators, precision=lax.Precision.HIGHEST).astype(jnp.bfloat16)
            summed = summed + spread.reshape(ANG, NU).astype(jnp.float32)
        return summed.astype(jnp.bfloat16)
    planes = lax.map(project_plane, volume)
    projection = jnp.transpose(planes, (1, 0, 2))
    norm_factor = 1.0 / math.sqrt(NZ * NU)
    lag_slices = jnp.arange(WZ, dtype=jnp.int32)
    lag_columns = jnp.arange(WU, dtype=jnp.int32)

    def correlate_slot(item):
        proj_slot, observed_slot_data, start_slice, start_col = item
        forward_spectrum = jnp.fft.fft2(proj_slot.astype(jnp.float32))
        observed_spectrum = jnp.fft.fft2(observed_slot_data.astype(jnp.float32))
        periodic_wrap = jnp.real(jnp.fft.ifft2(jnp.conj(forward_spectrum) * observed_spectrum))
        slice_rows = ((start_slice + lag_slices) % NZ).astype(jnp.int32)
        column_rows = ((start_col + lag_columns) % NU).astype(jnp.int32)
        return jnp.take(jnp.take(periodic_wrap, slice_rows, axis=0), column_rows, axis=1) * norm_factor
    correlation = lax.map(correlate_slot, (projection, measured, window_slice, window_col))
    weight_grid = correlation * correlation
    along_slices = (window_slice[:, None] + lag_slices[None, :]).astype(jnp.float32) / LAGZ
    along_columns = (window_col[:, None] + lag_columns[None, :]).astype(jnp.float32) / LAG
    denominator = lax.optimization_barrier(jnp.mean(weight_grid, axis=(1, 2))) + 1e-06
    shift_slices = lax.optimization_barrier(jnp.mean(weight_grid * along_slices[:, :, None], axis=(1, 2))) / denominator
    shift_columns = lax.optimization_barrier(jnp.mean(weight_grid * along_columns[:, None, :], axis=(1, 2))) / denominator
    return (projection, correlation, jnp.stack([shift_slices, shift_columns]))
```

```python
import functools
import math

import jax
import jax.numpy as jnp
from jax import lax
from jax.experimental import pallas as pl
from jax.experimental.pallas import tpu as pltpu
from jax.sharding import PartitionSpec as P

LAG = 32
WU = 16
LAGZ = 4
WZ = 4
GROUP = 16
CHUNKS = 4
MESH = pl.DeviceIdType.MESH


def loop(count, body):
    if count <= 32:
        for i in range(count):
            body(i)
    else:
        lax.fori_loop(0, count, lambda i, c: (body(i), c)[1], 0)


def kernel(
    slabs,
    cols,
    volume,
    weight,
    bank,
    tile_class,
    tile_shift,
    owner,
    measured,
    window_slice,
    window_col,
    projection,
    correlation,
    shifts,
    vol,
    meas,
    ray,
    send,
    recv,
    halo,
    mrows,
    mturn,
    plane,
    stage,
    parts,
    load_sem,
    meas_sem,
    send_sem,
    recv_sem,
    halo_send,
    halo_recv,
    part_send,
    part_recv,
    out_sem,
):
    slab, col = lax.axis_index("slab"), lax.axis_index("col")
    devices = slabs * cols
    me = slab * cols + col
    angles = weight.shape[0]
    size = bank.shape[1]
    columns = volume.shape[2]
    tiles = columns // size
    quarter = tiles // cols
    span = ray.shape[0] // angles
    right, left = lax.rem(col + 1, cols), lax.rem(col + cols - 1, cols)

    width = columns // CHUNKS
    loads = [
        pltpu.make_async_copy(
            volume.at[0, :, pl.ds(i * width, width)],
            vol.at[:, pl.ds(i * width, width)],
            load_sem.at[i],
        )
        for i in range(CHUNKS)
    ]
    for load in loads:
        load.start()
    meas_copy = pltpu.make_async_copy(measured.at[0], meas, meas_sem)
    meas_copy.start()

    barrier = pltpu.get_barrier_semaphore()

    def greet(i):
        peer = lax.rem(me + 1 + i, devices)
        pl.semaphore_signal(
            barrier, inc=1, device_id=(peer // cols, lax.rem(peer, cols)), device_id_type=MESH
        )

    loop(devices - 1, greet)

    for i in range(CHUNKS):
        loads[i].wait()
        sums = jnp.dot(
            weight[...], vol[:, i * width : (i + 1) * width], preferred_element_type=jnp.float32
        )
        for t in range(width // size):
            piece = sums[:, t * size : (t + 1) * size]
            tile = i * (width // size) + t
            for at in range(tile, span, tiles):
                ray[pl.ds(at, angles, stride=span), :] = piece

    def gather(k):
        angle = owner[k]
        opening = angle * span + tiles - tile_shift[angle]
        for c in range(cols):
            rows = ray[pl.ds(opening + c * quarter, GROUP), :]
            send[k * cols + c] = rows.astype(jnp.bfloat16)

    loop(angles, gather)

    pl.semaphore_wait(barrier, devices - 1)

    meas_copy.wait()
    halos = [
        pltpu.make_async_remote_copy(
            src_ref=meas.at[:, pl.ds((quarter - 1) * size, size)],
            dst_ref=halo.at[0],
            send_sem=halo_send.at[0],
            recv_sem=halo_recv.at[0],
            device_id=(slab, right),
            device_id_type=MESH,
        ),
        pltpu.make_async_remote_copy(
            src_ref=meas.at[:, pl.ds(0, size)],
            dst_ref=halo.at[1],
            send_sem=halo_send.at[1],
            recv_sem=halo_recv.at[1],
            device_id=(slab, left),
            device_id_type=MESH,
        ),
    ]

    def pass_on(i):
        peer = lax.rem(me + 1 + i, devices)
        pltpu.make_async_remote_copy(
            src_ref=send.at[peer],
            dst_ref=recv.at[col * slabs + slab],
            send_sem=send_sem,
            recv_sem=recv_sem,
            device_id=(peer // cols, lax.rem(peer, cols)),
            device_id_type=MESH,
        ).start()

    loop(devices - 1, pass_on)
    pltpu.make_async_copy(send.at[me], recv.at[col * slabs + slab], recv_sem).start()
    for copy in halos:
        copy.start()

    depth = slabs * GROUP
    mrows[...] = jnp.zeros_like(mrows)

    def put(which, row, tile):
        for copy in range(3):
            start = (which * 3 + copy) * depth + row
            mrows[pl.ds(start, slabs, stride=GROUP), :] = tile

    for t in range(quarter):
        tile = meas[:, t * size : (t + 1) * size].astype(jnp.float32)
        put(0, t, tile)
        if t > 0:
            put(1, t - 1, tile)
        if t < quarter - 1:
            put(2, t + 1, tile)
    for copy in halos:
        copy.wait()
    put(2, 0, halo[0].astype(jnp.float32))
    put(1, quarter - 1, halo[1].astype(jnp.float32))
    first_slice = window_slice[0]
    for a in range(WZ):
        opening = (first_slice + a + slabs) * GROUP
        for which in range(3):
            rows = mrows[pl.ds(which * 3 * depth + opening, depth), :]
            mturn[pl.ds((a * 3 + which) * size, size), :] = rows.T.astype(jnp.bfloat16)

    matrix = bank[tile_class[owner[slab]]]
    pltpu.make_async_copy(recv, recv, recv_sem).wait()

    pieces = recv[...].reshape(devices * GROUP, size)
    spread = jnp.dot(pieces, matrix, preferred_element_type=jnp.float32)
    spread = spread.astype(jnp.bfloat16).astype(jnp.float32)
    total = spread[:depth]
    for j in range(1, cols):
        total = total + spread[j * depth : (j + 1) * depth]
    rounded = total.astype(jnp.bfloat16)
    plane[...] = rounded.astype(jnp.float32)

    products = jnp.dot(mturn[...], rounded, preferred_element_type=jnp.float32)
    ahead = lax.broadcasted_iota(jnp.int32, (size, size), 0) - lax.broadcasted_iota(
        jnp.int32, (size, size), 1
    )
    sublane = lax.broadcasted_iota(jnp.int32, (8, size), 0)
    row = lax.broadcasted_iota(jnp.int32, (8, size), 0)
    lags = jnp.zeros((8, size), jnp.float32)
    for a in range(WZ):
        same, after, before = (
            products[(a * 3 + which) * size : (a * 3 + which + 1) * size] for which in range(3)
        )
        block = jnp.where(
            ahead >= size // 2, before, jnp.where(ahead < -(size // 2), after, same)
        )
        lanes = block[:8]
        for i in range(1, size // 8):
            lanes = lanes + pltpu.roll(block[8 * i : 8 * i + 8], size - 8 * i, 1)
        for bit in (1, 2, 4):
            lanes = jnp.where((sublane & bit) != 0, pltpu.roll(lanes, size - bit, 1), lanes)
        summed = jnp.sum(lanes, axis=0, keepdims=True)
        lags = jnp.where(row == a, summed, lags)
    parts[col] = lags

    others = []
    for i in range(1, cols):
        copy = pltpu.make_async_remote_copy(
            src_ref=parts.at[col],
            dst_ref=parts.at[col],
            send_sem=part_send.at[i - 1],
            recv_sem=part_recv.at[i - 1],
            device_id=(slab, lax.rem(col + i, cols)),
            device_id_type=MESH,
        )
        copy.start()
        others.append(copy)

    for t in range(quarter):
        stage[:, t * size : (t + 1) * size] = plane[pl.ds(t, slabs, stride=GROUP), :].astype(
            jnp.bfloat16
        )
    out_copy = pltpu.make_async_copy(stage, projection.at[0], out_sem)
    out_copy.start()

    first_col = window_col[0]
    place = lax.broadcasted_iota(jnp.int32, (size, size), 0)
    lane = lax.broadcasted_iota(jnp.int32, (size, size), 1)
    chosen = ((place + lane + first_col) & (size - 1)) == 0
    chosen = jnp.where(chosen, 1.0, 0.0)

    for copy in others:
        copy.wait()
    whole = parts[0]
    for j in range(1, cols):
        whole = whole + parts[j]
    norm = 1.0 / math.sqrt(slabs * columns)
    window = (
        jnp.dot(
            whole, chosen, precision=lax.Precision.HIGHEST, preferred_element_type=jnp.float32
        )
        * norm
    )
    correlation[0] = window[:WZ, :WU]
    column = lax.broadcasted_iota(jnp.int32, (8, size), 1)
    inside = (row < WZ) & (column < WU)
    grid = jnp.where(inside, window * window, 0.0)
    along_slices = (first_slice + row).astype(jnp.float32) / LAGZ
    along_columns = (first_col + column).astype(jnp.float32) / LAG
    count = WZ * WU

    def mean(value):
        return jnp.sum(jnp.sum(value, axis=1, keepdims=True), axis=0, keepdims=True) / count

    denominator = mean(grid) + 1e-06
    shifts[0:1, :] = mean(grid * along_slices) / denominator
    shifts[1:2, :] = mean(grid * along_columns) / denominator

    out_copy.wait()
    sent = send.at[pl.ds(0, devices - 1)]
    pltpu.make_async_copy(sent, sent, send_sem).wait()


def local(slabs, cols, *args):
    volume, weight, bank = args[:3]
    measured = args[6]
    _, beam_rows, columns = volume.shape
    angles = weight.shape[0]
    size = bank.shape[1]
    tiles = columns // size
    devices = slabs * cols
    depth = slabs * GROUP
    span = 2 * tiles + 8
    any_space = pl.BlockSpec(memory_space=pl.ANY)
    vmem = pl.BlockSpec(memory_space=pltpu.VMEM)
    smem = pl.BlockSpec(memory_space=pltpu.SMEM)
    dma = pltpu.SemaphoreType.DMA
    return pl.pallas_call(
        functools.partial(kernel, slabs, cols),
        out_shape=(
            jax.ShapeDtypeStruct(measured.shape, jnp.bfloat16),
            jax.ShapeDtypeStruct((1, WZ, WU), jnp.float32),
            jax.ShapeDtypeStruct((2, 1), jnp.float32),
        ),
        in_specs=[any_space, vmem, vmem, smem, smem, smem, any_space, smem, smem],
        out_specs=(any_space, vmem, vmem),
        scratch_shapes=[
            pltpu.VMEM((beam_rows, columns), jnp.bfloat16),
            pltpu.VMEM(measured.shape[1:], jnp.bfloat16),
            pltpu.VMEM((angles * span, size), jnp.float32),
            pltpu.VMEM((devices, GROUP, size), jnp.bfloat16),
            pltpu.VMEM((devices, GROUP, size), jnp.bfloat16),
            pltpu.VMEM((2, slabs, size), jnp.bfloat16),
            pltpu.VMEM((9 * depth, size), jnp.float32),
            pltpu.VMEM((3 * WZ * size, depth), jnp.bfloat16),
            pltpu.VMEM((depth, size), jnp.float32),
            pltpu.VMEM(measured.shape[1:], jnp.bfloat16),
            pltpu.VMEM((cols, 8, size), jnp.float32),
            dma((CHUNKS,)),
            dma,
            dma,
            dma,
            dma((2,)),
            dma((2,)),
            dma((cols - 1,)),
            dma((cols - 1,)),
            dma,
        ],
        compiler_params=pltpu.CompilerParams(
            collective_id=0, has_side_effects=True, vmem_limit_bytes=60 * 1024 * 1024
        ),
    )(*args)


def solution(mesh):
    slabs, cols = mesh.shape["slab"], mesh.shape["col"]
    return jax.shard_map(
        functools.partial(local, slabs, cols),
        mesh=mesh,
        in_specs=(
            P("slab", "col", None),
            P(None, "col"),
            P(),
            P(),
            P(),
            P(),
            P("slab", None, "col"),
            P("slab"),
            P("slab"),
        ),
        out_specs=(P("slab", None, "col"), P("slab", None, None), P(None, "slab")),
        check_vma=False,
    )
```

```python
import functools
import math

import jax
import jax.numpy as jnp
from jax import lax
from jax.experimental import pallas as pl
from jax.experimental.pallas import tpu as pltpu
from jax.sharding import PartitionSpec as P

LAG = 32
WU = 16
LAGZ = 4
WZ = 4
GROUP = 16
CHUNKS = 4
MESH = pl.DeviceIdType.MESH


def loop(count, body):
    if count <= 32:
        for i in range(count):
            body(i)
    else:
        lax.fori_loop(0, count, lambda i, c: (body(i), c)[1], 0)


def kernel(
    slabs,
    cols,
    volume,
    weight_in,
    bank_in,
    class_in,
    shift_in,
    owner_in,
    measured,
    window_slice,
    window_col,
    stage,
    parts,
    chosen,
    along,
    weight,
    bank,
    tile_class,
    tile_shift,
    owner,
    vol,
    meas,
    ray,
    send,
    recv,
    halo,
    mrows,
    mturn,
    plane,
    load_sem,
    small_sem,
    meas_sem,
    send_sem,
    recv_sem,
    halo_send,
    halo_recv,
    part_send,
    part_recv,
):
    slab, col = lax.axis_index("slab"), lax.axis_index("col")
    devices = slabs * cols
    me = slab * cols + col
    angles = weight.shape[0]
    size = bank.shape[1]
    columns = volume.shape[2]
    tiles = columns // size
    quarter = tiles // cols
    span = ray.shape[0] // angles
    right, left = lax.rem(col + 1, cols), lax.rem(col + cols - 1, cols)

    width = columns // CHUNKS
    loads = [
        pltpu.make_async_copy(
            volume.at[0, :, pl.ds(i * width, width)],
            vol.at[:, pl.ds(i * width, width)],
            load_sem.at[i],
        )
        for i in range(CHUNKS)
    ]
    pairs = (
        (weight_in, weight),
        (owner_in, owner),
        (shift_in, tile_shift),
        (class_in, tile_class),
        (bank_in, bank),
    )
    smalls = [
        pltpu.make_async_copy(source, target, small_sem.at[i])
        for i, (source, target) in enumerate(pairs)
    ]
    smalls[0].start()
    for load in loads:
        load.start()
    for small in smalls[1:]:
        small.start()
    meas_copy = pltpu.make_async_copy(measured.at[0], meas, meas_sem)
    meas_copy.start()

    barrier = pltpu.get_barrier_semaphore()

    def greet(i):
        peer = lax.rem(me + 1 + i, devices)
        pl.semaphore_signal(
            barrier, inc=1, device_id=(peer // cols, lax.rem(peer, cols)), device_id_type=MESH
        )

    loop(devices - 1, greet)

    smalls[0].wait()
    for i in range(CHUNKS):
        loads[i].wait()
        sums = jnp.dot(
            weight[...], vol[:, i * width : (i + 1) * width], preferred_element_type=jnp.float32
        )
        for t in range(width // size):
            piece = sums[:, t * size : (t + 1) * size]
            tile = i * (width // size) + t
            for at in range(tile, span, tiles):
                ray[pl.ds(at, angles, stride=span), :] = piece

    smalls[1].wait()
    smalls[2].wait()
    def gather(k):
        angle = owner[k]
        opening = angle * span + tiles - tile_shift[angle]
        for c in range(cols):
            rows = ray[pl.ds(opening + c * quarter, GROUP), :]
            send[k * cols + c] = rows.astype(jnp.bfloat16)

    loop(angles, gather)

    pl.semaphore_wait(barrier, devices - 1)

    meas_copy.wait()
    halos = [
        pltpu.make_async_remote_copy(
            src_ref=meas.at[:, pl.ds((quarter - 1) * size, size)],
            dst_ref=halo.at[0],
            send_sem=halo_send.at[0],
            recv_sem=halo_recv.at[0],
            device_id=(slab, right),
            device_id_type=MESH,
        ),
        pltpu.make_async_remote_copy(
            src_ref=meas.at[:, pl.ds(0, size)],
            dst_ref=halo.at[1],
            send_sem=halo_send.at[1],
            recv_sem=halo_recv.at[1],
            device_id=(slab, left),
            device_id_type=MESH,
        ),
    ]

    def pass_on(i):
        peer = lax.rem(me + 1 + i, devices)
        pltpu.make_async_remote_copy(
            src_ref=send.at[peer, pl.ds(0, quarter), :],
            dst_ref=recv.at[col * slabs + slab, pl.ds(0, quarter), :],
            send_sem=send_sem,
            recv_sem=recv_sem,
            device_id=(peer // cols, lax.rem(peer, cols)),
            device_id_type=MESH,
        ).start()

    loop(devices - 1, pass_on)
    pltpu.make_async_copy(
        send.at[me, pl.ds(0, quarter), :],
        recv.at[col * slabs + slab, pl.ds(0, quarter), :],
        recv_sem,
    ).start()
    for copy in halos:
        copy.start()

    depth = slabs * GROUP
    mrows[...] = jnp.zeros_like(mrows)

    def put(which, row, tile):
        for copy in range(3):
            start = (which * 3 + copy) * depth + row
            mrows[pl.ds(start, slabs, stride=GROUP), :] = tile

    for t in range(quarter):
        tile = meas[:, t * size : (t + 1) * size].astype(jnp.float32)
        put(0, t, tile)
        if t > 0:
            put(1, t - 1, tile)
        if t < quarter - 1:
            put(2, t + 1, tile)
    for copy in halos:
        copy.wait()
    put(2, 0, halo[0].astype(jnp.float32))
    put(1, quarter - 1, halo[1].astype(jnp.float32))
    first_slice = window_slice[0]
    for a in range(WZ):
        opening = (first_slice + a + slabs) * GROUP
        for which in range(3):
            rows = mrows[pl.ds(which * 3 * depth + opening, depth), :]
            mturn[pl.ds((a * 3 + which) * size, size), :] = rows.T.astype(jnp.bfloat16)

    first_col = window_col[0]
    place = lax.broadcasted_iota(jnp.int32, (size, size), 0)
    lane = lax.broadcasted_iota(jnp.int32, (size, size), 1)
    norm = 1.0 / math.sqrt(slabs * columns)
    inside = (((place + lane + first_col) & (size - 1)) == 0) & (lane < WU)
    chosen[...] = jnp.where(inside, norm, 0.0)
    row = lax.broadcasted_iota(jnp.int32, (8, size), 0)
    column = lax.broadcasted_iota(jnp.int32, (8, size), 1)
    along[0] = (first_slice + row).astype(jnp.float32) / LAGZ
    along[1] = (first_col + column).astype(jnp.float32) / LAG

    smalls[3].wait()
    smalls[4].wait()
    matrix = bank[tile_class[owner[slab]]]
    arrived = recv.at[:, pl.ds(0, quarter), :]
    pltpu.make_async_copy(arrived, arrived, recv_sem).wait()

    pieces = recv[...].reshape(devices * GROUP, size)
    spread = jnp.dot(pieces, matrix, preferred_element_type=jnp.float32)
    spread = spread.astype(jnp.bfloat16).astype(jnp.float32)
    total = spread[:depth]
    for j in range(1, cols):
        total = total + spread[j * depth : (j + 1) * depth]
    filled = lax.broadcasted_iota(jnp.int32, (depth, size), 0) & (GROUP - 1)
    rounded = jnp.where(filled < quarter, total, 0.0).astype(jnp.bfloat16)
    plane[...] = rounded.astype(jnp.float32)

    products = jnp.dot(mturn[...], rounded, preferred_element_type=jnp.float32)
    ahead = lax.broadcasted_iota(jnp.int32, (size, size), 0) - lax.broadcasted_iota(
        jnp.int32, (size, size), 1
    )
    sublane = lax.broadcasted_iota(jnp.int32, (8, size), 0)
    lags = jnp.zeros((8, size), jnp.float32)
    for a in range(WZ):
        same, after, before = (
            products[(a * 3 + which) * size : (a * 3 + which + 1) * size] for which in range(3)
        )
        block = jnp.where(
            ahead >= size // 2, before, jnp.where(ahead < -(size // 2), after, same)
        )
        lanes = block[:8]
        for i in range(1, size // 8):
            lanes = lanes + pltpu.roll(block[8 * i : 8 * i + 8], size - 8 * i, 1)
        for bit in (1, 2, 4):
            lanes = jnp.where((sublane & bit) != 0, pltpu.roll(lanes, size - bit, 1), lanes)
        summed = jnp.sum(lanes, axis=0, keepdims=True)
        lags = jnp.where(row == a, summed, lags)
    parts[col] = lags

    others = []
    for i in range(1, cols):
        copy = pltpu.make_async_remote_copy(
            src_ref=parts.at[col],
            dst_ref=parts.at[col],
            send_sem=part_send.at[i - 1],
            recv_sem=part_recv.at[i - 1],
            device_id=(slab, lax.rem(col + i, cols)),
            device_id_type=MESH,
        )
        copy.start()
        others.append(copy)

    for t in range(quarter):
        stage[:, t * size : (t + 1) * size] = plane[pl.ds(t, slabs, stride=GROUP), :].astype(
            jnp.bfloat16
        )
    for copy in others:
        copy.wait()
    sent = send.at[pl.ds(0, devices - 1), pl.ds(0, quarter), :]
    pltpu.make_async_copy(sent, sent, send_sem).wait()


def finish(stage, parts, chosen, along, projection, correlation, shifts, window, centre, sem):
    first = pltpu.make_async_copy(stage, projection.at[0], sem.at[0])
    first.start()
    whole = parts[0]
    for j in range(1, parts.shape[0]):
        whole = whole + parts[j]
    peaks = jnp.dot(
        whole,
        chosen[...],
        precision=lax.Precision.HIGHEST,
        preferred_element_type=jnp.float32,
    )
    window[0] = peaks[:WZ, :WU]
    second = pltpu.make_async_copy(window, correlation, sem.at[1])
    second.start()
    grid = peaks * peaks

    def mean(value):
        summed = jnp.sum(jnp.sum(value, axis=1, keepdims=True), axis=0, keepdims=True)
        return summed / (WZ * WU)

    denominator = mean(grid) + 1e-06
    centre[:, 0:1] = mean(grid * along[0]) / denominator
    centre[:, 1:2] = mean(grid * along[1]) / denominator
    third = pltpu.make_async_copy(centre, shifts, sem.at[2])
    third.start()
    first.wait()
    second.wait()
    third.wait()


def local(slabs, cols, *args):
    volume, weight, bank = args[:3]
    measured = args[6]
    _, beam_rows, columns = volume.shape
    angles = weight.shape[0]
    size = bank.shape[1]
    tiles = columns // size
    devices = slabs * cols
    depth = slabs * GROUP
    span = 2 * tiles + 8
    any_space = pl.BlockSpec(memory_space=pl.ANY)
    vmem = pl.BlockSpec(memory_space=pltpu.VMEM)
    dma = pltpu.SemaphoreType.DMA
    block = measured.shape[1:]
    scratch = [
        pltpu.VMEM(weight.shape, jnp.bfloat16),
        pltpu.VMEM(bank.shape, jnp.bfloat16),
        pltpu.SMEM(args[3].shape, jnp.int32),
        pltpu.SMEM(args[4].shape, jnp.int32),
        pltpu.SMEM(args[5].shape, jnp.int32),
        pltpu.VMEM((beam_rows, columns), jnp.bfloat16),
        pltpu.VMEM(block, jnp.bfloat16),
        pltpu.VMEM((angles * span, size), jnp.float32),
        pltpu.VMEM((devices, GROUP, size), jnp.bfloat16),
        pltpu.VMEM((devices, GROUP, size), jnp.bfloat16),
        pltpu.VMEM((2, slabs, size), jnp.bfloat16),
        pltpu.VMEM((9 * depth, size), jnp.float32),
        pltpu.VMEM((3 * WZ * size, depth), jnp.bfloat16),
        pltpu.VMEM((depth, size), jnp.float32),
    ]
    sums = pl.pallas_call(
        functools.partial(kernel, slabs, cols),
        out_shape=(
            pltpu.VMEM(block, jnp.bfloat16),
            pltpu.VMEM((cols, 8, size), jnp.float32),
            pltpu.VMEM((size, size), jnp.float32),
            pltpu.VMEM((2, 8, size), jnp.float32),
        ),
        in_specs=[any_space] * 7 + [pl.BlockSpec(memory_space=pltpu.SMEM)] * 2,
        out_specs=(vmem, vmem, vmem, vmem),
        scratch_shapes=scratch
        + [
            dma((CHUNKS,)),
            dma((5,)),
            dma,
            dma,
            dma,
            dma((2,)),
            dma((2,)),
            dma((cols - 1,)),
            dma((cols - 1,)),
        ],
        compiler_params=pltpu.CompilerParams(
            collective_id=0,
            has_side_effects=True,
            vmem_limit_bytes=60 * 2**20,
        ),
    )(*args)
    projection, correlation, centre = pl.pallas_call(
        finish,
        out_shape=(
            jax.ShapeDtypeStruct(measured.shape, jnp.bfloat16),
            jax.ShapeDtypeStruct((1, WZ, WU), jnp.float32),
            jax.ShapeDtypeStruct((1, 2), jnp.float32),
        ),
        in_specs=[vmem] * 4,
        out_specs=(any_space, any_space, any_space),
        scratch_shapes=[
            pltpu.VMEM((1, WZ, WU), jnp.float32),
            pltpu.VMEM((1, 2), jnp.float32),
            dma((3,)),
        ],
        compiler_params=pltpu.CompilerParams(vmem_limit_bytes=16 * 2**20),
    )(*sums)
    return projection, correlation, centre.T


def solution(mesh):
    slabs, cols = mesh.shape["slab"], mesh.shape["col"]
    return jax.shard_map(
        functools.partial(local, slabs, cols),
        mesh=mesh,
        in_specs=(
            P("slab", "col", None),
            P(None, "col"),
            P(),
            P(),
            P(),
            P(),
            P("slab", None, "col"),
            P("slab"),
            P("slab"),
        ),
        out_specs=(P("slab", None, "col"), P("slab", None, None), P(None, "slab")),
        check_vma=False,
    )
```

```python
import functools
import math

import jax
import jax.numpy as jnp
from jax import lax
from jax.experimental import pallas as pl
from jax.experimental.pallas import tpu as pltpu
from jax.sharding import PartitionSpec as P

LAG = 32
WU = 16
LAGZ = 4
WZ = 4
GROUP = 16
CHUNKS = 2
MESH = pl.DeviceIdType.MESH


def loop(count, body):
    if count <= 32:
        for i in range(count):
            body(i)
    else:
        lax.fori_loop(0, count, lambda i, c: (body(i), c)[1], 0)


def kernel(
    slabs,
    cols,
    volume,
    weight_in,
    bank_in,
    class_in,
    shift_in,
    owner_in,
    measured,
    window_slice,
    window_col,
    stage,
    parts,
    chosen,
    along,
    weight,
    bank,
    tile_class,
    tile_shift,
    owner,
    vol,
    meas,
    ray,
    send,
    recv,
    halo,
    mrows,
    mturn,
    plane,
    load_sem,
    small_sem,
    meas_sem,
    send_sem,
    recv_sem,
    halo_send,
    halo_recv,
    part_send,
    part_recv,
):
    slab, col = lax.axis_index("slab"), lax.axis_index("col")
    devices = slabs * cols
    me = slab * cols + col
    angles = weight.shape[0]
    size = bank.shape[1]
    columns = volume.shape[2]
    tiles = columns // size
    quarter = tiles // cols
    span = ray.shape[0] // angles
    right, left = lax.rem(col + 1, cols), lax.rem(col + cols - 1, cols)

    barrier = pltpu.get_barrier_semaphore()

    def greet(i):
        peer = lax.rem(me + 1 + i, devices)
        pl.semaphore_signal(
            barrier, inc=1, device_id=(peer // cols, lax.rem(peer, cols)), device_id_type=MESH
        )

    loop(devices - 1, greet)

    width = columns // CHUNKS
    loads = [
        pltpu.make_async_copy(
            volume.at[0, :, pl.ds(i * width, width)],
            vol.at[:, pl.ds(i * width, width)],
            load_sem.at[i],
        )
        for i in range(CHUNKS)
    ]
    pairs = (
        (weight_in, weight),
        (owner_in, owner),
        (shift_in, tile_shift),
        (class_in, tile_class),
        (bank_in, bank),
    )
    smalls = [
        pltpu.make_async_copy(source, target, small_sem.at[i])
        for i, (source, target) in enumerate(pairs)
    ]
    smalls[0].start()
    for load in loads:
        load.start()
    for small in smalls[1:]:
        small.start()
    meas_copy = pltpu.make_async_copy(measured.at[0], meas, meas_sem)
    meas_copy.start()


    smalls[0].wait()
    for i in range(CHUNKS):
        loads[i].wait()
        sums = jnp.dot(
            weight[...], vol[:, i * width : (i + 1) * width], preferred_element_type=jnp.float32
        )
        for t in range(width // size):
            piece = sums[:, t * size : (t + 1) * size]
            tile = i * (width // size) + t
            for at in range(tile, span, tiles):
                ray[pl.ds(at, angles, stride=span), :] = piece

    smalls[1].wait()
    smalls[2].wait()
    def gather(k):
        angle = owner[k]
        opening = angle * span + tiles - tile_shift[angle]
        for c in range(cols):
            rows = ray[pl.ds(opening + c * quarter, GROUP), :]
            send[k * cols + c] = rows.astype(jnp.bfloat16)

    loop(angles, gather)

    pl.semaphore_wait(barrier, devices - 1)

    meas_copy.wait()
    halos = [
        pltpu.make_async_remote_copy(
            src_ref=meas.at[:, pl.ds((quarter - 1) * size, size)],
            dst_ref=halo.at[0],
            send_sem=halo_send.at[0],
            recv_sem=halo_recv.at[0],
            device_id=(slab, right),
            device_id_type=MESH,
        ),
        pltpu.make_async_remote_copy(
            src_ref=meas.at[:, pl.ds(0, size)],
            dst_ref=halo.at[1],
            send_sem=halo_send.at[1],
            recv_sem=halo_recv.at[1],
            device_id=(slab, left),
            device_id_type=MESH,
        ),
    ]

    def pass_on(i):
        peer = lax.rem(me + 1 + i, devices)
        pltpu.make_async_remote_copy(
            src_ref=send.at[peer, pl.ds(0, quarter), :],
            dst_ref=recv.at[col * slabs + slab, pl.ds(0, quarter), :],
            send_sem=send_sem,
            recv_sem=recv_sem,
            device_id=(peer // cols, lax.rem(peer, cols)),
            device_id_type=MESH,
        ).start()

    loop(devices - 1, pass_on)
    pltpu.make_async_copy(
        send.at[me, pl.ds(0, quarter), :],
        recv.at[col * slabs + slab, pl.ds(0, quarter), :],
        recv_sem,
    ).start()
    for copy in halos:
        copy.start()

    depth = slabs * GROUP
    mrows[...] = jnp.zeros_like(mrows)

    def put(which, row, tile):
        for copy in range(3):
            start = (which * 3 + copy) * depth + row
            mrows[pl.ds(start, slabs, stride=GROUP), :] = tile

    for t in range(quarter):
        tile = meas[:, t * size : (t + 1) * size].astype(jnp.float32)
        put(0, t, tile)
        if t > 0:
            put(1, t - 1, tile)
        if t < quarter - 1:
            put(2, t + 1, tile)
    for copy in halos:
        copy.wait()
    put(2, 0, halo[0].astype(jnp.float32))
    put(1, quarter - 1, halo[1].astype(jnp.float32))
    first_slice = window_slice[0]
    for a in range(WZ):
        opening = (first_slice + a + slabs) * GROUP
        for which in range(3):
            rows = mrows[pl.ds(which * 3 * depth + opening, depth), :]
            mturn[pl.ds((a * 3 + which) * size, size), :] = rows.T.astype(jnp.bfloat16)

    first_col = window_col[0]
    place = lax.broadcasted_iota(jnp.int32, (size, size), 0)
    lane = lax.broadcasted_iota(jnp.int32, (size, size), 1)
    norm = 1.0 / math.sqrt(slabs * columns)
    inside = (((place + lane + first_col) & (size - 1)) == 0) & (lane < WU)
    chosen[...] = jnp.where(inside, norm, 0.0)
    row = lax.broadcasted_iota(jnp.int32, (8, size), 0)
    column = lax.broadcasted_iota(jnp.int32, (8, size), 1)
    along[0] = (first_slice + row).astype(jnp.float32) / LAGZ
    along[1] = (first_col + column).astype(jnp.float32) / LAG

    smalls[3].wait()
    smalls[4].wait()
    matrix = bank[tile_class[owner[slab]]]
    arrived = recv.at[:, pl.ds(0, quarter), :]
    pltpu.make_async_copy(arrived, arrived, recv_sem).wait()

    pieces = recv[...].reshape(devices * GROUP, size)
    spread = jnp.dot(pieces, matrix, preferred_element_type=jnp.float32)
    spread = spread.astype(jnp.bfloat16).astype(jnp.float32)
    total = spread[:depth]
    for j in range(1, cols):
        total = total + spread[j * depth : (j + 1) * depth]
    filled = lax.broadcasted_iota(jnp.int32, (depth, size), 0) & (GROUP - 1)
    rounded = jnp.where(filled < quarter, total, 0.0).astype(jnp.bfloat16)
    plane[...] = rounded.astype(jnp.float32)

    products = jnp.dot(mturn[...], rounded, preferred_element_type=jnp.float32)
    ahead = lax.broadcasted_iota(jnp.int32, (size, size), 0) - lax.broadcasted_iota(
        jnp.int32, (size, size), 1
    )
    sublane = lax.broadcasted_iota(jnp.int32, (8, size), 0)
    lags = jnp.zeros((8, size), jnp.float32)
    for a in range(WZ):
        same, after, before = (
            products[(a * 3 + which) * size : (a * 3 + which + 1) * size] for which in range(3)
        )
        block = jnp.where(
            ahead >= size // 2, before, jnp.where(ahead < -(size // 2), after, same)
        )
        lanes = block[:8]
        for i in range(1, size // 8):
            lanes = lanes + pltpu.roll(block[8 * i : 8 * i + 8], size - 8 * i, 1)
        for bit in (1, 2, 4):
            lanes = jnp.where((sublane & bit) != 0, pltpu.roll(lanes, size - bit, 1), lanes)
        summed = jnp.sum(lanes, axis=0, keepdims=True)
        lags = jnp.where(row == a, summed, lags)
    parts[col] = lags

    others = []
    for i in range(1, cols):
        copy = pltpu.make_async_remote_copy(
            src_ref=parts.at[col],
            dst_ref=parts.at[col],
            send_sem=part_send.at[i - 1],
            recv_sem=part_recv.at[i - 1],
            device_id=(slab, lax.rem(col + i, cols)),
            device_id_type=MESH,
        )
        copy.start()
        others.append(copy)

    for t in range(quarter):
        stage[:, t * size : (t + 1) * size] = plane[pl.ds(t, slabs, stride=GROUP), :].astype(
            jnp.bfloat16
        )
    for copy in others:
        copy.wait()
    sent = send.at[pl.ds(0, devices - 1), pl.ds(0, quarter), :]
    pltpu.make_async_copy(sent, sent, send_sem).wait()


def finish(stage, parts, chosen, along, projection, correlation, shifts, window, centre, sem):
    first = pltpu.make_async_copy(stage, projection.at[0], sem.at[0])
    first.start()
    whole = parts[0]
    for j in range(1, parts.shape[0]):
        whole = whole + parts[j]
    peaks = jnp.dot(
        whole,
        chosen[...],
        precision=lax.Precision.HIGHEST,
        preferred_element_type=jnp.float32,
    )
    window[0] = peaks[:WZ, :WU]
    second = pltpu.make_async_copy(window, correlation, sem.at[1])
    second.start()
    grid = peaks * peaks

    def mean(value):
        summed = jnp.sum(jnp.sum(value, axis=1, keepdims=True), axis=0, keepdims=True)
        return summed / (WZ * WU)

    denominator = mean(grid) + 1e-06
    centre[:, 0:1] = mean(grid * along[0]) / denominator
    centre[:, 1:2] = mean(grid * along[1]) / denominator
    third = pltpu.make_async_copy(centre, shifts, sem.at[2])
    third.start()
    first.wait()
    second.wait()
    third.wait()


def local(slabs, cols, *args):
    volume, weight, bank = args[:3]
    measured = args[6]
    _, beam_rows, columns = volume.shape
    angles = weight.shape[0]
    size = bank.shape[1]
    tiles = columns // size
    devices = slabs * cols
    depth = slabs * GROUP
    span = 2 * tiles + 8
    any_space = pl.BlockSpec(memory_space=pl.ANY)
    vmem = pl.BlockSpec(memory_space=pltpu.VMEM)
    dma = pltpu.SemaphoreType.DMA
    block = measured.shape[1:]
    scratch = [
        pltpu.VMEM(weight.shape, jnp.bfloat16),
        pltpu.VMEM(bank.shape, jnp.bfloat16),
        pltpu.SMEM(args[3].shape, jnp.int32),
        pltpu.SMEM(args[4].shape, jnp.int32),
        pltpu.SMEM(args[5].shape, jnp.int32),
        pltpu.VMEM((beam_rows, columns), jnp.bfloat16),
        pltpu.VMEM(block, jnp.bfloat16),
        pltpu.VMEM((angles * span, size), jnp.float32),
        pltpu.VMEM((devices, GROUP, size), jnp.bfloat16),
        pltpu.VMEM((devices, GROUP, size), jnp.bfloat16),
        pltpu.VMEM((2, slabs, size), jnp.bfloat16),
        pltpu.VMEM((9 * depth, size), jnp.float32),
        pltpu.VMEM((3 * WZ * size, depth), jnp.bfloat16),
        pltpu.VMEM((depth, size), jnp.float32),
    ]
    sums = pl.pallas_call(
        functools.partial(kernel, slabs, cols),
        out_shape=(
            pltpu.VMEM(block, jnp.bfloat16),
            pltpu.VMEM((cols, 8, size), jnp.float32),
            pltpu.VMEM((size, size), jnp.float32),
            pltpu.VMEM((2, 8, size), jnp.float32),
        ),
        in_specs=[any_space] * 7 + [pl.BlockSpec(memory_space=pltpu.SMEM)] * 2,
        out_specs=(vmem, vmem, vmem, vmem),
        scratch_shapes=scratch
        + [
            dma((CHUNKS,)),
            dma((5,)),
            dma,
            dma,
            dma,
            dma((2,)),
            dma((2,)),
            dma((cols - 1,)),
            dma((cols - 1,)),
        ],
        compiler_params=pltpu.CompilerParams(
            collective_id=0,
            has_side_effects=True,
            vmem_limit_bytes=60 * 2**20,
        ),
    )(*args)
    projection, correlation, centre = pl.pallas_call(
        finish,
        out_shape=(
            jax.ShapeDtypeStruct(measured.shape, jnp.bfloat16),
            jax.ShapeDtypeStruct((1, WZ, WU), jnp.float32),
            jax.ShapeDtypeStruct((1, 2), jnp.float32),
        ),
        in_specs=[vmem] * 4,
        out_specs=(any_space, any_space, any_space),
        scratch_shapes=[
            pltpu.VMEM((1, WZ, WU), jnp.float32),
            pltpu.VMEM((1, 2), jnp.float32),
            dma((3,)),
        ],
        compiler_params=pltpu.CompilerParams(vmem_limit_bytes=16 * 2**20),
    )(*sums)
    return projection, correlation, centre.T


def solution(mesh):
    slabs, cols = mesh.shape["slab"], mesh.shape["col"]
    return jax.shard_map(
        functools.partial(local, slabs, cols),
        mesh=mesh,
        in_specs=(
            P("slab", "col", None),
            P(None, "col"),
            P(),
            P(),
            P(),
            P(),
            P("slab", None, "col"),
            P("slab"),
            P("slab"),
        ),
        out_specs=(P("slab", None, "col"), P("slab", None, None), P(None, "slab")),
        check_vma=False,
    )
```
